32 devices in a mesh: grp: 2 (over y), occ: 4 (over z), aux: 4 (over x, core).
Axes of the slice: x: 2, y: 2, z: 4, core: 2. Of those that a mesh axis runs over, the one named last changes fastest.
Arguments:
- factors: float32 [8192, 3072], P(('grp', 'aux'), 'occ'), parts along dimension 0, may hold values from -0.75 to 0.75
- eps_occ: float32 [32], P('grp'), parts along dimension 0, may hold values from -2 to -0.5
- eps_vir: float32 [6144], P('grp'), parts along dimension 0, may hold values from 0.2 to 3
- tile_index: int32 [2], P('grp'), parts along dimension 0, may hold values from 0 to 15
- pair_offset: int32 [2], P('grp'), parts along dimension 0, may hold values from 1 to 3
Outputs:
- gradient: float32 [8192, 3072], P(('grp', 'aux'), 'occ'), parts along dimension 0
The draws below stay inside these ranges and needn't reach their ends.
There are 2 independent parts, one for each index of `grp`. The reference program is written for one: setup_inputs(seed, part) draws one part's arguments, and reference() takes and returns one part's arrays. A program takes and returns all parts, laid end to end along the dimension named above; each array names one. Nothing has to cross between parts.
All inputs are finite; a program needn't handle non-finite values.
Results may differ from the reference program's by a relative error of at most 0.0001.
Values sent between devices are 32-bit elements; how exact they have to be, the bound alone decides.
A program may use at most 64 MiB of HBM per device.

```python
import jax
import jax.numpy as jnp
from jax import lax

NAUX = 4096
VT = 192
NVIRT = 3072
BLK = 4
DMAX = 3
STEPS = 1
OCC = 16


def shard_levels(rng, dims, split, least, high):
    level = 1.0
    for position, blocks in split:
        steps = jax.random.uniform(jax.random.fold_in(jax.random.fold_in(rng, 6), position), (blocks,), jnp.float32, least / len(split), high / len(split))
        level = level * jnp.repeat(jnp.exp(steps), dims[position] // blocks).reshape((-1,) + (1,) * (len(dims) - 1 - position))
    return level


def bell_draw(key, shape, scale, bound, shards=(), kind=jnp.bfloat16):
    factor_of = shard_levels(key, shape, shards, -0.22, 0.18) if shards else 1.0
    entries = jax.random.normal(key, shape, jnp.float32) * scale * factor_of
    return jnp.minimum(jnp.maximum(entries, -bound), bound).astype(kind)


def setup_inputs(seed: int = 0, part: int = 0) -> dict:
    arg_keys = jax.random.split(jax.random.key(seed), 6)
    part_keys = jax.random.split(jax.random.fold_in(arg_keys[5], part), 6)
    factors = bell_draw(part_keys[0], (NAUX, OCC * VT), 0.125, 0.75, ((0, 4), (1, 4)), jnp.float32)
    eps_occ = jnp.clip(jax.random.uniform(part_keys[1], (OCC,), jnp.float32, -2.0, -0.5), -2.0, -0.5)
    eps_vir = jnp.clip(jax.random.uniform(part_keys[2], (NVIRT,), jnp.float32, 0.2, 3.0), 0.2, 3.0)
    tile_index = jax.random.randint(part_keys[3], (1,), 0, NVIRT // VT).astype(jnp.int32)
    pair_offset = jax.random.randint(part_keys[4], (STEPS,), 1, DMAX + 1).astype(jnp.int32)
    return {"factors": factors, "eps_occ": eps_occ, "eps_vir": eps_vir, "tile_index": tile_index, "pair_offset": pair_offset}


PRECISE = lax.Precision.HIGHEST


def inner_dot(left, right):
    return lax.dot_general(left, right, (((0,), (0,)), ((), ())), precision=PRECISE, preferred_element_type=jnp.float32)


def reference(factors, eps_occ, eps_vir, tile_index, pair_offset):
    tile_width = BLK * VT
    block_count = eps_occ.shape[0] // BLK
    blocks = factors.reshape(NAUX, block_count, tile_width).transpose(1, 0, 2)
    vir_energy = lax.dynamic_slice_in_dim(eps_vir, tile_index[0].astype(jnp.int32) * VT, VT)
    gaps = (vir_energy[None, None, :] - eps_occ.reshape(block_count, BLK)[:, :, None]).reshape(block_count, tile_width)
    gradient = jnp.zeros((block_count, NAUX, tile_width), jnp.float32)
    block_ids = jnp.arange(block_count, dtype=jnp.int32)
    for step_index in range(STEPS):
        partner_ids = ((block_ids - pair_offset[step_index]) % block_count).astype(jnp.int32)

        def pair_terms(block_id):
            partner_id = partner_ids[block_id]
            own_rows = blocks[block_id]
            far_rows = blocks[partner_id]
            pair_ints = inner_dot(own_rows, far_rows)
            amplitude = pair_ints / (gaps[block_id][:, None] + gaps[partner_id][None, :])
            own_grad = jnp.dot(far_rows, amplitude.T, precision=PRECISE, preferred_element_type=jnp.float32)
            far_grad = jnp.dot(own_rows, amplitude, precision=PRECISE, preferred_element_type=jnp.float32)
            return own_grad, far_grad

        own_grad, far_grad = lax.map(pair_terms, block_ids)
        gradient = gradient + own_grad
        gradient = gradient.at[partner_ids].add(far_grad)
    return gradient.transpose(1, 0, 2).reshape(NAUX, block_count * tile_width)
```

```python
import jax
import jax.numpy as jnp
from jax import lax
from jax.sharding import PartitionSpec as P

VT = 192
BLK = 4
DMAX = 3
CHUNKS = 4
LINE = 4

PRECISE = lax.Precision.HIGH


def inner_dot(left, right):
    return lax.dot_general(
        left, right, (((0,), (0,)), ((), ())), precision=PRECISE, preferred_element_type=jnp.float32
    )


def outer_dot(left, right):
    return lax.dot_general(
        left, right, (((1,), (1,)), ((), ())), precision=PRECISE, preferred_element_type=jnp.float32
    )


def gaps_of(vir_energy, energies):
    return (vir_energy[None, :] - energies[:, None]).reshape(-1)


def amplitude_of(own, far, own_gaps, far_gaps, weight):
    aux_count = lax.axis_size("aux")
    aux_rank = lax.axis_index("aux")
    share = far.shape[1] // aux_count
    ints = lax.psum_scatter(inner_dot(far, own), "aux", scatter_dimension=0, tiled=True)
    gaps = lax.dynamic_slice_in_dim(far_gaps, aux_rank * share, share)
    amplitude = jnp.where(weight > 0, weight * (ints / (gaps[:, None] + own_gaps[None, :])), 0.0)
    return lax.all_gather(amplitude, "aux", axis=0, tiled=True)


def term(far, amplitude):
    return jnp.dot(far, amplitude, precision=PRECISE, preferred_element_type=jnp.float32)


def local_ring(factors, eps_occ, eps_vir, tile_index, pair_offset):
    count = lax.axis_size("occ")
    me = lax.axis_index("occ")
    vir_energy = lax.dynamic_slice_in_dim(eps_vir, tile_index[0] * VT, VT)
    energy = eps_occ.reshape(count, BLK)
    own_gaps = gaps_of(vir_energy, energy[me])
    offset = pair_offset[0]
    total = jnp.zeros_like(factors)
    for sign in (1, -1):
        far = factors
        held = factors
        for hop in range(1, DMAX + 1):
            held = lax.ppermute(held, "occ", [(i, (i + sign) % count) for i in range(count)])
            far = jnp.where(offset == hop, held, far)
        far_gaps = gaps_of(vir_energy, energy[(me - sign * offset) % count])
        total = total + term(far, amplitude_of(factors, far, own_gaps, far_gaps, jnp.float32(1)))
    return total


def local_line(factors, eps_occ, eps_vir, tile_index, pair_offset):
    count = lax.axis_size("occ")
    me = lax.axis_index("occ")
    vir_energy = lax.dynamic_slice_in_dim(eps_vir, tile_index[0] * VT, VT)
    energy = eps_occ.reshape(count, BLK)
    own_gaps = gaps_of(vir_energy, energy[me])
    odd = pair_offset[0] % 2 == 1
    inner = (me == 1) | (me == 2)
    lower = lax.ppermute(factors, "occ", [(i, i + 1) for i in range(count - 1)])
    upper = lax.ppermute(factors, "occ", [(i + 1, i) for i in range(count - 1)])
    near = jnp.where(me % 2 == 0, upper, lower)
    other = jnp.where(me % 2 == 0, lower, upper)
    near_block = jnp.where(me % 2 == 0, me + 1, me - 1)
    near_gaps = gaps_of(vir_energy, energy[near_block])
    near_amp = amplitude_of(factors, near, own_gaps, near_gaps, jnp.where(odd, 1.0, 0.0))
    total = term(near, near_amp)
    far_block = jnp.where(odd, jnp.where(me % 2 == 0, me - 1, me + 1), me + 2) % count
    far_gaps = gaps_of(vir_energy, energy[far_block])
    weight = jnp.where(odd, 1.0, 2.0)
    width = factors.shape[1] // CHUNKS
    for chunk in range(CHUNKS):
        cols = slice(chunk * width, (chunk + 1) * width)
        across = lax.ppermute(near[:, cols], "occ", [(1, 2), (2, 1)])
        relay = jnp.where(odd, across, other[:, cols])
        ends = lax.ppermute(relay, "occ", [(2, 3), (1, 0)])
        far = jnp.where(inner, jnp.where(odd, other[:, cols], across), ends)
        amp = amplitude_of(factors, far, own_gaps, far_gaps[cols], weight)
        total = total + term(far, amp)
    return total


def solution(mesh):
    in_specs = (P(("grp", "aux"), "occ"), P("grp"), P("grp"), P("grp"), P("grp"))
    out_specs = P(("grp", "aux"), "occ")
    body = local_line if mesh.shape["occ"] == LINE else local_ring
    return jax.shard_map(body, mesh=mesh, in_specs=in_specs, out_specs=out_specs, check_vma=False)
```

```python
import functools

import jax
import jax.numpy as jnp
from jax import lax
from jax.experimental import pallas as pl
from jax.experimental.pallas import tpu as pltpu
from jax.sharding import PartitionSpec as P

VT = 192
BLK = 4
DMAX = 3
WIDTH = 128
LINE = 4
SHARDS = 4
MESH = pl.DeviceIdType.MESH

PRECISE = lax.Precision.HIGH


def inner_dot(left, right):
    return lax.dot_general(
        left, right, (((0,), (0,)), ((), ())), precision=PRECISE, preferred_element_type=jnp.float32
    )


def outer_dot(left, right):
    return lax.dot_general(
        left, right, (((1,), (1,)), ((), ())), precision=PRECISE, preferred_element_type=jnp.float32
    )


def gaps_of(vir_energy, energies):
    return (vir_energy[None, :] - energies[:, None]).reshape(-1)


def amplitude_of(own, far, own_gaps, far_gaps, weight):
    aux_count = lax.axis_size("aux")
    aux_rank = lax.axis_index("aux")
    share = far.shape[1] // aux_count
    ints = lax.psum_scatter(inner_dot(far, own), "aux", scatter_dimension=0, tiled=True)
    gaps = lax.dynamic_slice_in_dim(far_gaps, aux_rank * share, share)
    amplitude = jnp.where(weight > 0, weight * (ints / (gaps[:, None] + own_gaps[None, :])), 0.0)
    return lax.all_gather(amplitude, "aux", axis=0, tiled=True)


def term(far, amplitude):
    return jnp.dot(far, amplitude, precision=PRECISE, preferred_element_type=jnp.float32)


def local_ring(factors, eps_occ, eps_vir, tile_index, pair_offset):
    count = lax.axis_size("occ")
    me = lax.axis_index("occ")
    vir_energy = lax.dynamic_slice_in_dim(eps_vir, tile_index[0] * VT, VT)
    energy = eps_occ.reshape(count, BLK)
    own_gaps = gaps_of(vir_energy, energy[me])
    offset = pair_offset[0]
    total = jnp.zeros_like(factors)
    for sign in (1, -1):
        far = factors
        held = factors
        for hop in range(1, DMAX + 1):
            held = lax.ppermute(held, "occ", [(i, (i + sign) % count) for i in range(count)])
            far = jnp.where(offset == hop, held, far)
        far_gaps = gaps_of(vir_energy, energy[(me - sign * offset) % count])
        total = total + term(far, amplitude_of(factors, far, own_gaps, far_gaps, jnp.float32(1)))
    return total


def split(x):
    high = x.astype(jnp.bfloat16)
    return high, (x - high.astype(jnp.float32)).astype(jnp.bfloat16)


def dot3(left, right, dims):
    dot = functools.partial(lax.dot_general, dimension_numbers=(dims, ((), ())), preferred_element_type=jnp.float32)
    return dot(left[0], right[0]) + (dot(left[0], right[1]) + dot(left[1], right[0]))


def line_kernel(
    occ, aux, own, odd_ref, own_gaps, gaps, weights, out,
    near, other, across, relay, own_hi, own_lo, far_hi, far_lo,
    ints, core_in, half, x_in, amp,
    near_s, near_r, other_s, other_r, fwd_s, relay_s, across_r,
    a_s, a_r, b_s, b_r, c_s, c_r,
):
    chunks, rows, width = near.shape
    tile_width = own.shape[1]
    share = width // 2
    me = lax.axis_index("occ")
    rank = lax.axis_index("aux")
    inner = jnp.logical_and(me > 0, me < occ - 1)
    side = {"occ": me + 1 - 2 * (me % 2)}
    middle = {"occ": occ - 1 - me}
    core = {"aux": rank + 1 - 2 * (rank % 2)}
    xpeer = {"aux": (rank + 2) % aux}
    mine = pl.multiple_of((rank % 2) * share, share)
    theirs = pl.multiple_of((1 - rank % 2) * share, share)

    def remote(src, dst, send, recv, target):
        return pltpu.make_async_remote_copy(
            src_ref=src, dst_ref=dst, send_sem=send, recv_sem=recv, device_id=target, device_id_type=MESH
        )

    def columns(c):
        return pl.ds(pl.multiple_of(c * width, width), width)

    def near_copy(c):
        return remote(own.at[:, columns(c)], near.at[c], near_s.at[c], near_r.at[c], side)

    def other_copy(c):
        return remote(own.at[:, columns(c)], other.at[c], other_s.at[c], other_r.at[c], middle)

    def forward_copy(c):
        return remote(near.at[c], across.at[c], fwd_s.at[c], across_r.at[c], middle)

    def relay_copy(c):
        return remote(relay.at[c], across.at[c], relay_s.at[c], across_r.at[c], side)

    def a_copy(i):
        return remote(ints.at[i, pl.ds(theirs, share)], core_in.at[i], a_s.at[i], a_r.at[i], core)

    def b_copy(i):
        return remote(half.at[i], x_in.at[i], b_s.at[i], b_r.at[i], xpeer)

    def c_copy(i):
        rows_of = amp.at[i, pl.ds(mine, share)]
        return remote(rows_of, rows_of, c_s.at[i], c_r.at[i], core)

    barrier = pltpu.get_barrier_semaphore()
    for target in (side, core, xpeer):
        pl.semaphore_signal(barrier, inc=1, device_id=target, device_id_type=MESH)

    @pl.when(inner)
    def _():
        pl.semaphore_signal(barrier, inc=1, device_id=middle, device_id_type=MESH)
        pl.semaphore_wait(barrier, 4)

    @pl.when(jnp.logical_not(inner))
    def _():
        pl.semaphore_wait(barrier, 3)

    @pl.loop(0, chunks)
    def _(c):
        near_copy(c).start()

        @pl.when(inner)
        def _():
            other_copy(c).start()

    band = 256

    @pl.loop(0, rows // band)
    def _(t):
        span = pl.ds(pl.multiple_of(t * band, band), band)
        own_hi[span, :], own_lo[span, :] = split(own[span, :])
        out[span, :] = jnp.zeros((band, tile_width), jnp.float32)

    def store_far(slot, span, far):
        far_hi[slot, span, :], far_lo[slot, span, :] = split(far)

    def front(i, slot):
        c = i % chunks

        @pl.when(i < chunks)
        def _():
            near_copy(c).wait_recv()

            @pl.when(inner)
            def _():
                forward_copy(c).start()

            @pl.loop(0, rows // band)
            def _(t):
                span = pl.ds(pl.multiple_of(t * band, band), band)
                store_far(slot, span, near[c, span, :])

        @pl.when(i >= chunks)
        def _():
            @pl.when(inner)
            def _():
                other_copy(c).wait_recv()
                forward_copy(c).wait_recv()
                odd = jnp.broadcast_to(odd_ref[...], (band, width)) > 0

                @pl.loop(0, rows // band)
                def _(t):
                    span = pl.ds(pl.multiple_of(t * band, band), band)
                    relay[c, span, :] = jnp.where(odd, across[c, span, :], other[c, span, :])

                relay_copy(c).start()

                @pl.loop(0, rows // band)
                def _(t):
                    span = pl.ds(pl.multiple_of(t * band, band), band)
                    store_far(slot, span, jnp.where(odd, other[c, span, :], across[c, span, :]))

            @pl.when(jnp.logical_not(inner))
            def _():
                relay_copy(c).wait_recv()

                @pl.loop(0, rows // band)
                def _(t):
                    span = pl.ds(pl.multiple_of(t * band, band), band)
                    store_far(slot, span, across[c, span, :])

        for n in range(0, tile_width, band):
            cols = slice(n, n + band)
            ints[i, :, cols] = dot3(
                (far_hi[slot], far_lo[slot]), (own_hi[:, cols], own_lo[:, cols]), ((0,), (0,))
            )
        a_copy(i).start()

    items = 2 * chunks

    @pl.loop(0, items + 1)
    def _(i):
        slot, back = i % 2, (i + 1) % 2

        @pl.when(i < items)
        def _():
            front(i, slot)

        @pl.when(i > 0)
        def _():
            j = i - 1
            b_copy(j).wait_recv()
            at = pl.ds(pl.multiple_of(j * width + mine, share), share)
            total = half[j] + x_in[j]
            amp[j, pl.ds(mine, share), :] = weights[at, :] * (total / (gaps[at, :] + own_gaps[...]))
            c_copy(j).start()

        @pl.when(i < items)
        def _():
            a_copy(i).wait_recv()
            half[i] = ints[i, pl.ds(mine, share), :] + core_in[i]
            b_copy(i).start()

        @pl.when(i > 0)
        def _():
            j = i - 1
            c_copy(j).wait_recv()
            amp_parts = split(amp[j])

            @pl.loop(0, rows // band)
            def _(t):
                span = pl.ds(pl.multiple_of(t * band, band), band)
                out[span, :] += dot3((far_hi[back, span, :], far_lo[back, span, :]), amp_parts, ((1,), (0,)))

    @pl.loop(0, chunks)
    def _(c):
        near_copy(c).wait_send()

        @pl.when(inner)
        def _():
            other_copy(c).wait_send()
            forward_copy(c).wait_send()
            relay_copy(c).wait_send()

    @pl.loop(0, items)
    def _(i):
        a_copy(i).wait_send()
        b_copy(i).wait_send()
        c_copy(i).wait_send()


def local_line(factors, eps_occ, eps_vir, tile_index, pair_offset):
    count = lax.axis_size("occ")
    aux_count = lax.axis_size("aux")
    me = lax.axis_index("occ")
    rows, tile_width = factors.shape
    vir_energy = lax.dynamic_slice_in_dim(eps_vir, tile_index[0] * VT, VT)
    energy = eps_occ.reshape(count, BLK)
    odd = pair_offset[0] % 2 == 1
    near_block = me + 1 - 2 * (me % 2)
    far_block = jnp.where(odd, jnp.where(me % 2 == 0, me - 1, me + 1), me + 2) % count
    own_gaps = gaps_of(vir_energy, energy[me]).reshape(1, tile_width)
    blocks = jnp.stack([energy[near_block], energy[far_block]]).reshape(2 * BLK)
    gaps = gaps_of(vir_energy, blocks).reshape(2 * tile_width, 1)
    scale = jnp.where(odd, 1.0, jnp.array([0.0, 2.0], jnp.float32))
    weights = jnp.repeat(scale, tile_width).reshape(2 * tile_width, 1)
    odd_row = jnp.full((1, WIDTH), odd, jnp.float32)
    chunks = tile_width // WIDTH
    items = 2 * chunks
    f32, half = jnp.float32, jnp.bfloat16
    block = pltpu.VMEM((chunks, rows, WIDTH), f32)
    share = pltpu.VMEM((items, WIDTH // 2, tile_width), f32)
    dma = pltpu.SemaphoreType.DMA
    vmem = pl.BlockSpec(memory_space=pltpu.VMEM)
    return pl.pallas_call(
        functools.partial(line_kernel, count, aux_count),
        out_shape=jax.ShapeDtypeStruct((rows, tile_width), f32),
        in_specs=[vmem] * 5,
        out_specs=vmem,
        scratch_shapes=[block] * 4
        + [pltpu.VMEM((rows, tile_width), half)] * 2
        + [pltpu.VMEM((2, rows, WIDTH), half)] * 2
        + [pltpu.VMEM((items, WIDTH, tile_width), f32), share, share, share]
        + [pltpu.VMEM((items, WIDTH, tile_width), f32)]
        + [dma((chunks,))] * 7
        + [dma((items,))] * 6,
        compiler_params=pltpu.CompilerParams(
            collective_id=0, has_side_effects=True, vmem_limit_bytes=56 * 1024 * 1024
        ),
        name="pair_line",
    )(factors, odd_row, own_gaps, gaps, weights)


def solution(mesh):
    in_specs = (P(("grp", "aux"), "occ"), P("grp"), P("grp"), P("grp"), P("grp"))
    out_specs = P(("grp", "aux"), "occ")
    body = local_line if mesh.shape["occ"] == LINE and mesh.shape["aux"] == SHARDS else local_ring
    return jax.shard_map(body, mesh=mesh, in_specs=in_specs, out_specs=out_specs, check_vma=False)
```

```python
import functools

import jax
import jax.numpy as jnp
from jax import lax
from jax.experimental import pallas as pl
from jax.experimental.pallas import tpu as pltpu
from jax.sharding import PartitionSpec as P

VT = 192
BLK = 4
DMAX = 3
WIDTH = 128
PARTS = 4
NTILE = 256
LINE = 4
SHARDS = 4
MESH = pl.DeviceIdType.MESH

PRECISE = lax.Precision.HIGH


def inner_dot(left, right):
    return lax.dot_general(
        left, right, (((0,), (0,)), ((), ())), precision=PRECISE, preferred_element_type=jnp.float32
    )


def outer_dot(left, right):
    return lax.dot_general(
        left, right, (((1,), (1,)), ((), ())), precision=PRECISE, preferred_element_type=jnp.float32
    )


def gaps_of(vir_energy, energies):
    return (vir_energy[None, :] - energies[:, None]).reshape(-1)


def amplitude_of(own, far, own_gaps, far_gaps, weight):
    aux_count = lax.axis_size("aux")
    aux_rank = lax.axis_index("aux")
    share = far.shape[1] // aux_count
    ints = lax.psum_scatter(inner_dot(far, own), "aux", scatter_dimension=0, tiled=True)
    gaps = lax.dynamic_slice_in_dim(far_gaps, aux_rank * share, share)
    amplitude = jnp.where(weight > 0, weight * (ints / (gaps[:, None] + own_gaps[None, :])), 0.0)
    return lax.all_gather(amplitude, "aux", axis=0, tiled=True)


def term(far, amplitude):
    return jnp.dot(far, amplitude, precision=PRECISE, preferred_element_type=jnp.float32)


def local_ring(factors, eps_occ, eps_vir, tile_index, pair_offset):
    count = lax.axis_size("occ")
    me = lax.axis_index("occ")
    vir_energy = lax.dynamic_slice_in_dim(eps_vir, tile_index[0] * VT, VT)
    energy = eps_occ.reshape(count, BLK)
    own_gaps = gaps_of(vir_energy, energy[me])
    offset = pair_offset[0]
    total = jnp.zeros_like(factors)
    for sign in (1, -1):
        far = factors
        held = factors
        for hop in range(1, DMAX + 1):
            held = lax.ppermute(held, "occ", [(i, (i + sign) % count) for i in range(count)])
            far = jnp.where(offset == hop, held, far)
        far_gaps = gaps_of(vir_energy, energy[(me - sign * offset) % count])
        total = total + term(far, amplitude_of(factors, far, own_gaps, far_gaps, jnp.float32(1)))
    return total


def split(x):
    high = x.astype(jnp.bfloat16)
    return high, (x - high.astype(jnp.float32)).astype(jnp.bfloat16)


def dot3(left, right, dims):
    dot = functools.partial(lax.dot_general, dimension_numbers=(dims, ((), ())), preferred_element_type=jnp.float32)
    return dot(left[0], right[0]) + (dot(left[0], right[1]) + dot(left[1], right[0]))


def line_kernel(
    occ, aux, own, offset, table, out,
    near, other, across, relay, own_hi, own_lo, far_hi, far_lo,
    ints, core_in, half, x_in, amp, own_row, gap_cols,
    near_s, near_r, other_s, other_r, fwd_s, relay_s, across_r,
    a_s, a_r, b_s, b_r, c_s, c_r,
):
    chunks, rows, width = near.shape
    tile_width = own.shape[1]
    share = width // 2
    band = rows // PARTS
    me = lax.axis_index("occ")
    rank = lax.axis_index("aux")
    inner = jnp.logical_and(me > 0, me < occ - 1)
    side = {"occ": me + 1 - 2 * (me % 2)}
    middle = {"occ": occ - 1 - me}
    core = {"aux": rank + 1 - 2 * (rank % 2)}
    xpeer = {"aux": (rank + 2) % aux}
    mine = pl.multiple_of((rank % 2) * share, share)
    theirs = pl.multiple_of((1 - rank % 2) * share, share)

    def remote(src, dst, send, recv, target):
        return pltpu.make_async_remote_copy(
            src_ref=src, dst_ref=dst, send_sem=send, recv_sem=recv, device_id=target, device_id_type=MESH
        )

    def columns(c):
        return pl.ds(pl.multiple_of(c * width, width), width)

    def near_copy(c):
        return remote(own.at[:, columns(c)], near.at[c], near_s.at[c], near_r.at[c], side)

    def other_copy(c):
        return remote(own.at[:, columns(c)], other.at[c], other_s.at[c], other_r.at[c], middle)

    def band_of(t):
        return pl.ds(pl.multiple_of(t * band, band), band)

    def forward_copy(c, t):
        span = band_of(t)
        return remote(near.at[c, span], across.at[c, span], fwd_s.at[c, t], across_r.at[c, t], middle)

    def relay_copy(c, t):
        span = band_of(t)
        return remote(relay.at[c, span], across.at[c, span], relay_s.at[c, t], across_r.at[c, t], side)

    def a_copy(i):
        return remote(ints.at[i, pl.ds(theirs, share)], core_in.at[i], a_s.at[i], a_r.at[i], core)

    def b_copy(i):
        return remote(half.at[i], x_in.at[i], b_s.at[i], b_r.at[i], xpeer)

    def c_copy(i):
        rows_of = amp.at[i, pl.ds(mine, share)]
        return remote(rows_of, rows_of, c_s.at[i], c_r.at[i], core)

    barrier = pltpu.get_barrier_semaphore()
    for target in (side, core, xpeer):
        pl.semaphore_signal(barrier, inc=1, device_id=target, device_id_type=MESH)

    @pl.when(inner)
    def _():
        pl.semaphore_signal(barrier, inc=1, device_id=middle, device_id_type=MESH)
        pl.semaphore_wait(barrier, 4)

    @pl.when(jnp.logical_not(inner))
    def _():
        pl.semaphore_wait(barrier, 3)

    @pl.loop(0, chunks)
    def _(c):
        near_copy(c).start()

        @pl.when(inner)
        def _():
            other_copy(c).start()

    items = 2 * chunks
    odd = offset[0] & 1

    @pl.loop(0, PARTS)
    def _(t):
        span = band_of(t)
        own_hi[span, :], own_lo[span, :] = split(own[span, :])
        out[span, :] = jnp.zeros((band, tile_width), jnp.float32)

    for r in range(chunks):
        own_row[:, r * width : (r + 1) * width] = table[r : r + 1, :]

    @pl.loop(0, items)
    def _(i):
        gap_cols[i] = jnp.broadcast_to(table[pl.ds(chunks + i, 1), :], (width, width)).T

    def pick(odd_one, even_one):
        return jnp.where(jnp.full((band, width), odd, jnp.int32) > 0, odd_one, even_one)

    def serve(c, t):
        @pl.when(inner)
        def _():
            if t == 0:
                other_copy(c).wait_recv()
            forward_copy(c, t).wait_recv()
            span = band_of(t)
            relay[c, span, :] = pick(across[c, span, :], other[c, span, :])
            relay_copy(c, t).start()

    def serve_next(i, t):
        @pl.when(jnp.logical_and(i >= chunks - 1, i < items - 1))
        def _():
            serve(i + 1 - chunks, t)

    def integrals(i, slot, t, far):
        span = band_of(t)
        parts = split(far)
        far_hi[slot, span, :], far_lo[slot, span, :] = parts
        for n in range(0, tile_width, NTILE):
            cols = slice(n, n + NTILE)
            ints[i, :, cols] += dot3(parts, (own_hi[span, cols], own_lo[span, cols]), ((0,), (0,)))

    def front(i, slot):
        c = i % chunks
        ints[i] = jnp.zeros((width, tile_width), jnp.float32)

        @pl.when(i < chunks)
        def _():
            near_copy(c).wait_recv()

            @pl.when(inner)
            def _():
                @pl.loop(0, PARTS)
                def _(t):
                    forward_copy(c, t).start()

            @pl.loop(0, PARTS)
            def _(t):
                integrals(i, slot, t, near[c, band_of(t), :])

        @pl.when(i >= chunks)
        def _():
            serve(c, PARTS - 1)

            @pl.when(inner)
            def _():
                @pl.loop(0, PARTS)
                def _(t):
                    span = band_of(t)
                    integrals(i, slot, t, pick(other[c, span, :], across[c, span, :]))

            @pl.when(jnp.logical_not(inner))
            def _():
                @pl.loop(0, PARTS)
                def _(t):
                    relay_copy(c, t).wait_recv()
                    integrals(i, slot, t, across[c, band_of(t), :])

        a_copy(i).start()

    @pl.loop(0, items + 1)
    def _(i):
        slot, back = i % 2, (i + 1) % 2

        @pl.when(i < items)
        def _():
            front(i, slot)

        serve_next(i, 0)

        @pl.when(i > 0)
        def _():
            j = i - 1
            b_copy(j).wait_recv()
            at = pl.ds(mine, share)
            single = jnp.full((share, width), odd, jnp.int32).astype(jnp.float32)
            weight = jnp.where(j < chunks, single, 2.0 - single)
            for r in range(chunks):
                cols = slice(r * width, (r + 1) * width)
                total = half[j, :, cols] + x_in[j, :, cols]
                amp[j, at, cols] = weight * (total / (gap_cols[j, at, :] + own_row[:, cols]))
            c_copy(j).start()

        @pl.when(i < items)
        def _():
            a_copy(i).wait_recv()
            half[i] = ints[i, pl.ds(mine, share), :] + core_in[i]
            b_copy(i).start()

        serve_next(i, 1)

        @pl.when(i > 0)
        def _():
            j = i - 1
            c_copy(j).wait_recv()

        def add_terms(first, last):
            @pl.when(i > 0)
            def _():
                amp_parts = split(amp[i - 1])

                @pl.loop(first, last)
                def _(t):
                    span = band_of(t)
                    out[span, :] += dot3((far_hi[back, span, :], far_lo[back, span, :]), amp_parts, ((1,), (0,)))

        add_terms(0, PARTS // 2)
        serve_next(i, 2)
        add_terms(PARTS // 2, PARTS)

    @pl.loop(0, chunks)
    def _(c):
        near_copy(c).wait_send()

        @pl.when(inner)
        def _():
            other_copy(c).wait_send()

            @pl.loop(0, PARTS)
            def _(t):
                forward_copy(c, t).wait_send()
                relay_copy(c, t).wait_send()

    @pl.loop(0, items)
    def _(i):
        a_copy(i).wait_send()
        b_copy(i).wait_send()
        c_copy(i).wait_send()


def local_line(factors, eps_occ, eps_vir, tile_index, pair_offset):
    count = lax.axis_size("occ")
    aux_count = lax.axis_size("aux")
    me = lax.axis_index("occ")
    rows, tile_width = factors.shape
    vir_energy = lax.dynamic_slice_in_dim(eps_vir, tile_index[0] * VT, VT)
    energy = eps_occ.reshape(count, BLK)
    odd = pair_offset[0] % 2 == 1
    near_block = me + 1 - 2 * (me % 2)
    far_block = jnp.where(odd, jnp.where(me % 2 == 0, me - 1, me + 1), me + 2) % count
    blocks = jnp.stack([energy[me], energy[near_block], energy[far_block]]).reshape(3 * BLK)
    table = gaps_of(vir_energy, blocks).reshape(3 * tile_width // WIDTH, WIDTH)
    chunks = tile_width // WIDTH
    items = 2 * chunks
    f32, half = jnp.float32, jnp.bfloat16
    block = pltpu.VMEM((chunks, rows, WIDTH), f32)
    share = pltpu.VMEM((items, WIDTH // 2, tile_width), f32)
    dma = pltpu.SemaphoreType.DMA
    vmem = pl.BlockSpec(memory_space=pltpu.VMEM)
    return pl.pallas_call(
        functools.partial(line_kernel, count, aux_count),
        out_shape=jax.ShapeDtypeStruct((rows, tile_width), f32),
        in_specs=[vmem, pl.BlockSpec(memory_space=pltpu.SMEM), vmem],
        out_specs=vmem,
        scratch_shapes=[block] * 4
        + [pltpu.VMEM((rows, tile_width), half)] * 2
        + [pltpu.VMEM((2, rows, WIDTH), half)] * 2
        + [pltpu.VMEM((items, WIDTH, tile_width), f32), share, share, share]
        + [pltpu.VMEM((items, WIDTH, tile_width), f32)]
        + [pltpu.VMEM((1, tile_width), f32), pltpu.VMEM((items, WIDTH, WIDTH), f32)]
        + [dma((chunks,))] * 4
        + [dma((chunks, PARTS))] * 3
        + [dma((items,))] * 6,
        compiler_params=pltpu.CompilerParams(
            collective_id=0, has_side_effects=True, vmem_limit_bytes=56 * 1024 * 1024
        ),
        name="pair_line",
    )(factors, pair_offset, table)


def solution(mesh):
    in_specs = (P(("grp", "aux"), "occ"), P("grp"), P("grp"), P("grp"), P("grp"))
    out_specs = P(("grp", "aux"), "occ")
    body = local_line if mesh.shape["occ"] == LINE and mesh.shape["aux"] == SHARDS else local_ring
    return jax.shard_map(body, mesh=mesh, in_specs=in_specs, out_specs=out_specs, check_vma=False)
```

```python
import functools

import jax
import jax.numpy as jnp
from jax import lax
from jax.experimental import pallas as pl
from jax.experimental.pallas import tpu as pltpu
from jax.sharding import PartitionSpec as P

VT = 192
BLK = 4
DMAX = 3
WIDTH = 128
PARTS = 4
SLOTS = 3
NTILE = 256
LINE = 4
SHARDS = 4
MESH = pl.DeviceIdType.MESH

PRECISE = lax.Precision.HIGH


def inner_dot(left, right):
    return lax.dot_general(
        left, right, (((0,), (0,)), ((), ())), precision=PRECISE, preferred_element_type=jnp.float32
    )


def outer_dot(left, right):
    return lax.dot_general(
        left, right, (((1,), (1,)), ((), ())), precision=PRECISE, preferred_element_type=jnp.float32
    )


def gaps_of(vir_energy, energies):
    return (vir_energy[None, :] - energies[:, None]).reshape(-1)


def amplitude_of(own, far, own_gaps, far_gaps, weight):
    aux_count = lax.axis_size("aux")
    aux_rank = lax.axis_index("aux")
    share = far.shape[1] // aux_count
    ints = lax.psum_scatter(inner_dot(far, own), "aux", scatter_dimension=0, tiled=True)
    gaps = lax.dynamic_slice_in_dim(far_gaps, aux_rank * share, share)
    amplitude = jnp.where(weight > 0, weight * (ints / (gaps[:, None] + own_gaps[None, :])), 0.0)
    return lax.all_gather(amplitude, "aux", axis=0, tiled=True)


def term(far, amplitude):
    return jnp.dot(far, amplitude, precision=PRECISE, preferred_element_type=jnp.float32)


def local_ring(factors, eps_occ, eps_vir, tile_index, pair_offset):
    count = lax.axis_size("occ")
    me = lax.axis_index("occ")
    vir_energy = lax.dynamic_slice_in_dim(eps_vir, tile_index[0] * VT, VT)
    energy = eps_occ.reshape(count, BLK)
    own_gaps = gaps_of(vir_energy, energy[me])
    offset = pair_offset[0]
    total = jnp.zeros_like(factors)
    for sign in (1, -1):
        far = factors
        held = factors
        for hop in range(1, DMAX + 1):
            held = lax.ppermute(held, "occ", [(i, (i + sign) % count) for i in range(count)])
            far = jnp.where(offset == hop, held, far)
        far_gaps = gaps_of(vir_energy, energy[(me - sign * offset) % count])
        total = total + term(far, amplitude_of(factors, far, own_gaps, far_gaps, jnp.float32(1)))
    return total


def split(x):
    high = x.astype(jnp.bfloat16)
    return high, (x - high.astype(jnp.float32)).astype(jnp.bfloat16)


def dot3(left, right, dims):
    dot = functools.partial(lax.dot_general, dimension_numbers=(dims, ((), ())), preferred_element_type=jnp.float32)
    return dot(left[0], right[0]) + (dot(left[0], right[1]) + dot(left[1], right[0]))


def line_kernel(
    occ, aux, own, offset, table, total_out, far_out, amp_out, out,
    near, other, across, relay, own_hi, own_lo, far_hi, far_lo,
    ints, core_in, half, x_in, amp, own_row, gap_cols,
    near_s, near_r, other_s, other_r, fwd_s, relay_s, across_r,
    a_s, a_r, b_s, b_r, c_s, c_r, out_s,
):
    chunks, rows, width = near.shape
    tile_width = own.shape[1]
    share = width // 2
    band = rows // PARTS
    me = lax.axis_index("occ")
    rank = lax.axis_index("aux")
    inner = jnp.logical_and(me > 0, me < occ - 1)
    side = {"occ": me + 1 - 2 * (me % 2)}
    middle = {"occ": occ - 1 - me}
    core = {"aux": rank + 1 - 2 * (rank % 2)}
    xpeer = {"aux": (rank + 2) % aux}
    mine = pl.multiple_of((rank % 2) * share, share)
    theirs = pl.multiple_of((1 - rank % 2) * share, share)

    def remote(src, dst, send, recv, target):
        return pltpu.make_async_remote_copy(
            src_ref=src, dst_ref=dst, send_sem=send, recv_sem=recv, device_id=target, device_id_type=MESH
        )

    def columns(c):
        return pl.ds(pl.multiple_of(c * width, width), width)

    def near_copy(c):
        return remote(own.at[:, columns(c)], near.at[c], near_s.at[c], near_r.at[c], side)

    def other_copy(c):
        return remote(own.at[:, columns(c)], other.at[c], other_s.at[c], other_r.at[c], middle)

    def band_of(t):
        return pl.ds(pl.multiple_of(t * band, band), band)

    def forward_copy(c, t):
        span = band_of(t)
        return remote(near.at[c, span], across.at[c, span], fwd_s.at[c, t], across_r.at[c, t], middle)

    def relay_copy(c, t):
        span = band_of(t)
        return remote(relay.at[c, span], across.at[c, span], relay_s.at[c, t], across_r.at[c, t], side)

    def a_copy(i):
        return remote(ints.at[i, pl.ds(theirs, share)], core_in.at[i], a_s.at[i], a_r.at[i], core)

    def b_copy(i):
        return remote(half.at[i], x_in.at[i], b_s.at[i], b_r.at[i], xpeer)

    def c_copy(i):
        rows_of = amp.at[i, pl.ds(mine, share)]
        return remote(rows_of, rows_of, c_s.at[i], c_r.at[i], core)

    barrier = pltpu.get_barrier_semaphore()
    for target in (side, core, xpeer):
        pl.semaphore_signal(barrier, inc=1, device_id=target, device_id_type=MESH)

    @pl.when(inner)
    def _():
        pl.semaphore_signal(barrier, inc=1, device_id=middle, device_id_type=MESH)
        pl.semaphore_wait(barrier, 4)

    @pl.when(jnp.logical_not(inner))
    def _():
        pl.semaphore_wait(barrier, 3)

    @pl.loop(0, chunks)
    def _(c):
        near_copy(c).start()

        @pl.when(inner)
        def _():
            other_copy(c).start()

    items = 2 * chunks
    odd = offset[0] & 1

    @pl.loop(0, PARTS)
    def _(t):
        span = band_of(t)
        own_hi[span, :], own_lo[span, :] = split(own[span, :])
        out[span, :] = jnp.zeros((band, tile_width), jnp.float32)

    for r in range(chunks):
        own_row[:, r * width : (r + 1) * width] = table[r : r + 1, :]

    @pl.loop(0, items)
    def _(i):
        gap_cols[i] = jnp.broadcast_to(table[pl.ds(chunks + i, 1), :], (width, width)).T

    def pick(odd_one, even_one):
        return jnp.where(jnp.full((band, width), odd, jnp.int32) > 0, odd_one, even_one)

    def integrals(i, slot, t, far):
        span = band_of(t)
        parts = split(far)
        far_hi[slot, span, :], far_lo[slot, span, :] = parts

        @pl.when(i == items - 1)
        def _():
            far_out[span, :] = far

        for n in range(0, tile_width, NTILE):
            cols = slice(n, n + NTILE)
            ints[i, :, cols] += dot3(parts, (own_hi[span, cols], own_lo[span, cols]), ((0,), (0,)))

    def serve(c, t):
        @pl.when(inner)
        def _():
            if t == 0:
                other_copy(c).wait_recv()
            forward_copy(c, t).wait_recv()
            span = band_of(t)
            relay[c, span, :] = pick(across[c, span, :], other[c, span, :])
            relay_copy(c, t).start()
            i = c + chunks
            if t == 0:
                ints[i] = jnp.zeros((width, tile_width), jnp.float32)
            integrals(i, i % SLOTS, t, pick(other[c, span, :], across[c, span, :]))

    def serve_next(i, t):
        @pl.when(jnp.logical_and(i >= chunks - 1, i < items - 1))
        def _():
            serve(i + 1 - chunks, t)

    def front(i, slot):
        c = i % chunks

        @pl.when(i < chunks)
        def _():
            ints[i] = jnp.zeros((width, tile_width), jnp.float32)
            near_copy(c).wait_recv()

            @pl.when(inner)
            def _():
                @pl.loop(0, PARTS)
                def _(t):
                    forward_copy(c, t).start()

            @pl.loop(0, PARTS)
            def _(t):
                integrals(i, slot, t, near[c, band_of(t), :])

        @pl.when(i >= chunks)
        def _():
            serve(c, PARTS - 1)

            @pl.when(jnp.logical_not(inner))
            def _():
                ints[i] = jnp.zeros((width, tile_width), jnp.float32)

                @pl.loop(0, PARTS)
                def _(t):
                    relay_copy(c, t).wait_recv()
                    integrals(i, slot, t, across[c, band_of(t), :])

        a_copy(i).start()

    @pl.loop(0, items + 1)
    def _(i):
        slot, back = i % SLOTS, (i + SLOTS - 1) % SLOTS

        @pl.when(i == items)
        def _():
            pltpu.make_async_copy(out, total_out, out_s).start()

        @pl.when(i < items)
        def _():
            front(i, slot)

        serve_next(i, 0)

        @pl.when(i > 0)
        def _():
            j = i - 1
            b_copy(j).wait_recv()
            at = pl.ds(mine, share)
            single = jnp.full((share, width), odd, jnp.int32).astype(jnp.float32)
            weight = jnp.where(j < chunks, single, 2.0 - single)
            for r in range(chunks):
                cols = slice(r * width, (r + 1) * width)
                total = half[j, :, cols] + x_in[j, :, cols]
                amp[j, at, cols] = weight * (total / (gap_cols[j, at, :] + own_row[:, cols]))
            c_copy(j).start()

        @pl.when(i < items)
        def _():
            a_copy(i).wait_recv()
            half[i] = ints[i, pl.ds(mine, share), :] + core_in[i]
            b_copy(i).start()

        serve_next(i, 1)

        @pl.when(i > 0)
        def _():
            j = i - 1
            c_copy(j).wait_recv()

        def add_terms(first, last):
            @pl.when(jnp.logical_and(i > 0, i < items))
            def _():
                amp_parts = split(amp[i - 1])

                @pl.loop(first, last)
                def _(t):
                    span = band_of(t)
                    out[span, :] += dot3((far_hi[back, span, :], far_lo[back, span, :]), amp_parts, ((1,), (0,)))

        add_terms(0, PARTS // 2)
        serve_next(i, 2)
        add_terms(PARTS // 2, PARTS)

    amp_out[...] = amp[items - 1]
    pltpu.make_async_copy(out, total_out, out_s).wait()

    @pl.loop(0, chunks)
    def _(c):
        near_copy(c).wait_send()

        @pl.when(inner)
        def _():
            other_copy(c).wait_send()

            @pl.loop(0, PARTS)
            def _(t):
                forward_copy(c, t).wait_send()
                relay_copy(c, t).wait_send()

    @pl.loop(0, items)
    def _(i):
        a_copy(i).wait_send()
        b_copy(i).wait_send()
        c_copy(i).wait_send()


def local_line(factors, eps_occ, eps_vir, tile_index, pair_offset):
    count = lax.axis_size("occ")
    aux_count = lax.axis_size("aux")
    me = lax.axis_index("occ")
    rows, tile_width = factors.shape
    vir_energy = lax.dynamic_slice_in_dim(eps_vir, tile_index[0] * VT, VT)
    energy = eps_occ.reshape(count, BLK)
    odd = pair_offset[0] % 2 == 1
    near_block = me + 1 - 2 * (me % 2)
    far_block = jnp.where(odd, jnp.where(me % 2 == 0, me - 1, me + 1), me + 2) % count
    blocks = jnp.stack([energy[me], energy[near_block], energy[far_block]]).reshape(3 * BLK)
    table = gaps_of(vir_energy, blocks).reshape(3 * tile_width // WIDTH, WIDTH)
    chunks = tile_width // WIDTH
    items = 2 * chunks
    f32, half = jnp.float32, jnp.bfloat16
    block = pltpu.VMEM((chunks, rows, WIDTH), f32)
    share = pltpu.VMEM((items, WIDTH // 2, tile_width), f32)
    dma = pltpu.SemaphoreType.DMA
    vmem = pl.BlockSpec(memory_space=pltpu.VMEM)
    total, far, amplitude = pl.pallas_call(
        functools.partial(line_kernel, count, aux_count),
        out_shape=[
            jax.ShapeDtypeStruct((rows, tile_width), f32),
            jax.ShapeDtypeStruct((rows, WIDTH), f32),
            jax.ShapeDtypeStruct((WIDTH, tile_width), f32),
        ],
        in_specs=[vmem, pl.BlockSpec(memory_space=pltpu.SMEM), vmem],
        out_specs=[pl.BlockSpec(memory_space=pl.ANY), vmem, vmem],
        scratch_shapes=[pltpu.VMEM((rows, tile_width), f32)]
        + [block] * 4
        + [pltpu.VMEM((rows, tile_width), half)] * 2
        + [pltpu.VMEM((SLOTS, rows, WIDTH), half)] * 2
        + [pltpu.VMEM((items, WIDTH, tile_width), f32), share, share, share]
        + [pltpu.VMEM((items, WIDTH, tile_width), f32)]
        + [pltpu.VMEM((1, tile_width), f32), pltpu.VMEM((items, WIDTH, WIDTH), f32)]
        + [dma((chunks,))] * 4
        + [dma((chunks, PARTS))] * 3
        + [dma((items,))] * 6
        + [dma],
        compiler_params=pltpu.CompilerParams(
            collective_id=0, has_side_effects=True, vmem_limit_bytes=56 * 1024 * 1024
        ),
        name="pair_line",
    )(factors, pair_offset, table)
    return total + term(far, amplitude)


def solution(mesh):
    in_specs = (P(("grp", "aux"), "occ"), P("grp"), P("grp"), P("grp"), P("grp"))
    out_specs = P(("grp", "aux"), "occ")
    body = local_line if mesh.shape["occ"] == LINE and mesh.shape["aux"] == SHARDS else local_ring
    return jax.shard_map(body, mesh=mesh, in_specs=in_specs, out_specs=out_specs, check_vma=False)
```

```python
import functools

import jax
import jax.numpy as jnp
from jax import lax
from jax.experimental import pallas as pl
from jax.experimental.pallas import tpu as pltpu
from jax.sharding import PartitionSpec as P

VT = 192
BLK = 4
DMAX = 3
WIDTH = 128
PARTS = 4
SLOTS = 3
AHEAD = 2
NTILE = 256
LINE = 4
SHARDS = 4
MESH = pl.DeviceIdType.MESH

PRECISE = lax.Precision.HIGH


def inner_dot(left, right):
    return lax.dot_general(
        left, right, (((0,), (0,)), ((), ())), precision=PRECISE, preferred_element_type=jnp.float32
    )


def outer_dot(left, right):
    return lax.dot_general(
        left, right, (((1,), (1,)), ((), ())), precision=PRECISE, preferred_element_type=jnp.float32
    )


def gaps_of(vir_energy, energies):
    return (vir_energy[None, :] - energies[:, None]).reshape(-1)


def amplitude_of(own, far, own_gaps, far_gaps, weight):
    aux_count = lax.axis_size("aux")
    aux_rank = lax.axis_index("aux")
    share = far.shape[1] // aux_count
    ints = lax.psum_scatter(inner_dot(far, own), "aux", scatter_dimension=0, tiled=True)
    gaps = lax.dynamic_slice_in_dim(far_gaps, aux_rank * share, share)
    amplitude = jnp.where(weight > 0, weight * (ints / (gaps[:, None] + own_gaps[None, :])), 0.0)
    return lax.all_gather(amplitude, "aux", axis=0, tiled=True)


def term(far, amplitude):
    return jnp.dot(far, amplitude, precision=PRECISE, preferred_element_type=jnp.float32)


def local_ring(factors, eps_occ, eps_vir, tile_index, pair_offset):
    count = lax.axis_size("occ")
    me = lax.axis_index("occ")
    vir_energy = lax.dynamic_slice_in_dim(eps_vir, tile_index[0] * VT, VT)
    energy = eps_occ.reshape(count, BLK)
    own_gaps = gaps_of(vir_energy, energy[me])
    offset = pair_offset[0]
    total = jnp.zeros_like(factors)
    for sign in (1, -1):
        far = factors
        held = factors
        for hop in range(1, DMAX + 1):
            held = lax.ppermute(held, "occ", [(i, (i + sign) % count) for i in range(count)])
            far = jnp.where(offset == hop, held, far)
        far_gaps = gaps_of(vir_energy, energy[(me - sign * offset) % count])
        total = total + term(far, amplitude_of(factors, far, own_gaps, far_gaps, jnp.float32(1)))
    return total


def split(x):
    high = x.astype(jnp.bfloat16)
    return high, (x - high.astype(jnp.float32)).astype(jnp.bfloat16)


def dot3(left, right, dims):
    dot = functools.partial(lax.dot_general, dimension_numbers=(dims, ((), ())), preferred_element_type=jnp.float32)
    return dot(left[0], right[0]) + (dot(left[0], right[1]) + dot(left[1], right[0]))


def line_kernel(
    occ, aux, own, offset, table, total_out, far_out, amp_out, out,
    near, other, across, relay, own_hi, own_lo, far_hi, far_lo,
    ints, core_in, half, x_in, amp, own_row, gap_cols,
    near_s, near_r, other_s, other_r, fwd_s, relay_s, across_r,
    a_s, a_r, b_s, b_r, c_s, c_r, out_s,
):
    chunks, rows, width = near.shape
    tile_width = own.shape[1]
    share = width // 2
    band = rows // PARTS
    me = lax.axis_index("occ")
    rank = lax.axis_index("aux")
    inner = jnp.logical_and(me > 0, me < occ - 1)
    side = {"occ": me + 1 - 2 * (me % 2)}
    middle = {"occ": occ - 1 - me}
    core = {"aux": rank + 1 - 2 * (rank % 2)}
    xpeer = {"aux": (rank + 2) % aux}
    mine = pl.multiple_of((rank % 2) * share, share)
    theirs = pl.multiple_of((1 - rank % 2) * share, share)

    def remote(src, dst, send, recv, target):
        return pltpu.make_async_remote_copy(
            src_ref=src, dst_ref=dst, send_sem=send, recv_sem=recv, device_id=target, device_id_type=MESH
        )

    def columns(c):
        return pl.ds(pl.multiple_of(c * width, width), width)

    def near_copy(c):
        return remote(own.at[:, columns(c)], near.at[c], near_s.at[c], near_r.at[c], side)

    def other_copy(c):
        return remote(own.at[:, columns(c)], other.at[c], other_s.at[c], other_r.at[c], middle)

    def band_of(t):
        return pl.ds(pl.multiple_of(t * band, band), band)

    def forward_copy(c, t):
        span = band_of(t)
        return remote(near.at[c, span], across.at[c, span], fwd_s.at[c, t], across_r.at[c, t], middle)

    def relay_copy(c, t):
        span = band_of(t)
        return remote(relay.at[c, span], across.at[c, span], relay_s.at[c, t], across_r.at[c, t], side)

    def a_copy(i):
        return remote(ints.at[i, pl.ds(theirs, share)], core_in.at[i], a_s.at[i], a_r.at[i], core)

    def b_copy(i):
        return remote(half.at[i], x_in.at[i], b_s.at[i], b_r.at[i], xpeer)

    def c_copy(i):
        rows_of = amp.at[i, pl.ds(mine, share)]
        return remote(rows_of, rows_of, c_s.at[i], c_r.at[i], core)

    barrier = pltpu.get_barrier_semaphore()
    for target in (side, core, xpeer):
        pl.semaphore_signal(barrier, inc=1, device_id=target, device_id_type=MESH)

    @pl.when(inner)
    def _():
        pl.semaphore_signal(barrier, inc=1, device_id=middle, device_id_type=MESH)
        pl.semaphore_wait(barrier, 4)

    @pl.when(jnp.logical_not(inner))
    def _():
        pl.semaphore_wait(barrier, 3)

    @pl.loop(0, chunks)
    def _(c):
        near_copy(c).start()

        @pl.when(jnp.logical_and(inner, c < AHEAD))
        def _():
            other_copy(c).start()

    items = 2 * chunks
    odd = offset[0] & 1

    @pl.loop(0, PARTS)
    def _(t):
        span = band_of(t)
        own_hi[span, :], own_lo[span, :] = split(own[span, :])
        out[span, :] = jnp.zeros((band, tile_width), jnp.float32)

    for r in range(chunks):
        own_row[:, r * width : (r + 1) * width] = table[r : r + 1, :]

    @pl.loop(0, items)
    def _(i):
        gap_cols[i] = jnp.broadcast_to(table[pl.ds(chunks + i, 1), :], (width, width)).T

    def pick(odd_one, even_one):
        return jnp.where(jnp.full((band, width), odd, jnp.int32) > 0, odd_one, even_one)

    def integrals(i, slot, t, far):
        span = band_of(t)
        parts = split(far)
        far_hi[slot, span, :], far_lo[slot, span, :] = parts

        @pl.when(i == items - 1)
        def _():
            far_out[span, :] = far

        for n in range(0, tile_width, NTILE):
            cols = slice(n, n + NTILE)
            ints[i, :, cols] += dot3(parts, (own_hi[span, cols], own_lo[span, cols]), ((0,), (0,)))

    def serve(c, t):
        @pl.when(inner)
        def _():
            if t == 0:
                other_copy(c).wait_recv()
            forward_copy(c, t).wait_recv()
            span = band_of(t)
            relay[c, span, :] = pick(across[c, span, :], other[c, span, :])
            relay_copy(c, t).start()
            i = c + chunks
            if t == 0:
                ints[i] = jnp.zeros((width, tile_width), jnp.float32)
            integrals(i, i % SLOTS, t, pick(other[c, span, :], across[c, span, :]))

    def serve_next(i, t):
        @pl.when(jnp.logical_and(i >= chunks - 1, i < items - 1))
        def _():
            serve(i + 1 - chunks, t)

    def front(i, slot):
        c = i % chunks

        @pl.when(i < chunks)
        def _():
            ints[i] = jnp.zeros((width, tile_width), jnp.float32)
            near_copy(c).wait_recv()

            @pl.when(inner)
            def _():
                @pl.loop(0, PARTS)
                def _(t):
                    forward_copy(c, t).start()

                @pl.when(c + AHEAD < chunks)
                def _():
                    other_copy(c + AHEAD).start()

            @pl.loop(0, PARTS)
            def _(t):
                integrals(i, slot, t, near[c, band_of(t), :])

        @pl.when(i >= chunks)
        def _():
            serve(c, PARTS - 1)

            @pl.when(jnp.logical_not(inner))
            def _():
                ints[i] = jnp.zeros((width, tile_width), jnp.float32)

                @pl.loop(0, PARTS)
                def _(t):
                    relay_copy(c, t).wait_recv()
                    integrals(i, slot, t, across[c, band_of(t), :])

        a_copy(i).start()

    @pl.loop(0, items + 1)
    def _(i):
        slot, back = i % SLOTS, (i + SLOTS - 1) % SLOTS

        @pl.when(i == items)
        def _():
            pltpu.make_async_copy(out, total_out, out_s).start()

        @pl.when(i < items)
        def _():
            front(i, slot)

        serve_next(i, 0)

        @pl.when(i > 0)
        def _():
            j = i - 1
            b_copy(j).wait_recv()
            at = pl.ds(mine, share)
            single = jnp.full((share, width), odd, jnp.int32).astype(jnp.float32)
            weight = jnp.where(j < chunks, single, 2.0 - single)
            for r in range(chunks):
                cols = slice(r * width, (r + 1) * width)
                total = half[j, :, cols] + x_in[j, :, cols]
                amp[j, at, cols] = weight * (total / (gap_cols[j, at, :] + own_row[:, cols]))
            c_copy(j).start()

        @pl.when(i < items)
        def _():
            a_copy(i).wait_recv()
            half[i] = ints[i, pl.ds(mine, share), :] + core_in[i]
            b_copy(i).start()

        serve_next(i, 1)

        @pl.when(i > 0)
        def _():
            j = i - 1
            c_copy(j).wait_recv()

        def add_terms(first, last):
            @pl.when(jnp.logical_and(i > 0, i < items))
            def _():
                amp_parts = split(amp[i - 1])

                @pl.loop(first, last)
                def _(t):
                    span = band_of(t)
                    out[span, :] += dot3((far_hi[back, span, :], far_lo[back, span, :]), amp_parts, ((1,), (0,)))

        add_terms(0, PARTS // 2)
        serve_next(i, 2)
        add_terms(PARTS // 2, PARTS)

    amp_out[...] = amp[items - 1]
    pltpu.make_async_copy(out, total_out, out_s).wait()

    @pl.loop(0, chunks)
    def _(c):
        near_copy(c).wait_send()

        @pl.when(inner)
        def _():
            other_copy(c).wait_send()

            @pl.loop(0, PARTS)
            def _(t):
                forward_copy(c, t).wait_send()
                relay_copy(c, t).wait_send()

    @pl.loop(0, items)
    def _(i):
        a_copy(i).wait_send()
        b_copy(i).wait_send()
        c_copy(i).wait_send()


def local_line(factors, eps_occ, eps_vir, tile_index, pair_offset):
    count = lax.axis_size("occ")
    aux_count = lax.axis_size("aux")
    me = lax.axis_index("occ")
    rows, tile_width = factors.shape
    vir_energy = lax.dynamic_slice_in_dim(eps_vir, tile_index[0] * VT, VT)
    energy = eps_occ.reshape(count, BLK)
    odd = pair_offset[0] % 2 == 1
    near_block = me + 1 - 2 * (me % 2)
    far_block = jnp.where(odd, jnp.where(me % 2 == 0, me - 1, me + 1), me + 2) % count
    blocks = jnp.stack([energy[me], energy[near_block], energy[far_block]]).reshape(3 * BLK)
    table = gaps_of(vir_energy, blocks).reshape(3 * tile_width // WIDTH, WIDTH)
    chunks = tile_width // WIDTH
    items = 2 * chunks
    f32, half = jnp.float32, jnp.bfloat16
    block = pltpu.VMEM((chunks, rows, WIDTH), f32)
    share = pltpu.VMEM((items, WIDTH // 2, tile_width), f32)
    dma = pltpu.SemaphoreType.DMA
    vmem = pl.BlockSpec(memory_space=pltpu.VMEM)
    total, far, amplitude = pl.pallas_call(
        functools.partial(line_kernel, count, aux_count),
        out_shape=[
            jax.ShapeDtypeStruct((rows, tile_width), f32),
            jax.ShapeDtypeStruct((rows, WIDTH), f32),
            jax.ShapeDtypeStruct((WIDTH, tile_width), f32),
        ],
        in_specs=[vmem, pl.BlockSpec(memory_space=pltpu.SMEM), vmem],
        out_specs=[pl.BlockSpec(memory_space=pl.ANY), vmem, vmem],
        scratch_shapes=[pltpu.VMEM((rows, tile_width), f32)]
        + [block] * 4
        + [pltpu.VMEM((rows, tile_width), half)] * 2
        + [pltpu.VMEM((SLOTS, rows, WIDTH), half)] * 2
        + [pltpu.VMEM((items, WIDTH, tile_width), f32), share, share, share]
        + [pltpu.VMEM((items, WIDTH, tile_width), f32)]
        + [pltpu.VMEM((1, tile_width), f32), pltpu.VMEM((items, WIDTH, WIDTH), f32)]
        + [dma((chunks,))] * 4
        + [dma((chunks, PARTS))] * 3
        + [dma((items,))] * 6
        + [dma],
        compiler_params=pltpu.CompilerParams(
            collective_id=0, has_side_effects=True, vmem_limit_bytes=56 * 1024 * 1024
        ),
        name="pair_line",
    )(factors, pair_offset, table)
    return total + term(far, amplitude)


def solution(mesh):
    in_specs = (P(("grp", "aux"), "occ"), P("grp"), P("grp"), P("grp"), P("grp"))
    out_specs = P(("grp", "aux"), "occ")
    body = local_line if mesh.shape["occ"] == LINE and mesh.shape["aux"] == SHARDS else local_ring
    return jax.shard_map(body, mesh=mesh, in_specs=in_specs, out_specs=out_specs, check_vma=False)
```

```python
import functools

import jax
import jax.numpy as jnp
from jax import lax
from jax.experimental import pallas as pl
from jax.experimental.pallas import tpu as pltpu
from jax.sharding import PartitionSpec as P

VT = 192
BLK = 4
DMAX = 3
WIDTH = 128
PARTS = 4
SLOTS = 3
NTILE = 768
LINE = 4
SHARDS = 4
MESH = pl.DeviceIdType.MESH

PRECISE = lax.Precision.HIGH


def inner_dot(left, right):
    return lax.dot_general(
        left, right, (((0,), (0,)), ((), ())), precision=PRECISE, preferred_element_type=jnp.float32
    )


def outer_dot(left, right):
    return lax.dot_general(
        left, right, (((1,), (1,)), ((), ())), precision=PRECISE, preferred_element_type=jnp.float32
    )


def gaps_of(vir_energy, energies):
    return (vir_energy[None, :] - energies[:, None]).reshape(-1)


def amplitude_of(own, far, own_gaps, far_gaps, weight):
    aux_count = lax.axis_size("aux")
    aux_rank = lax.axis_index("aux")
    share = far.shape[1] // aux_count
    ints = lax.psum_scatter(inner_dot(far, own), "aux", scatter_dimension=0, tiled=True)
    gaps = lax.dynamic_slice_in_dim(far_gaps, aux_rank * share, share)
    amplitude = jnp.where(weight > 0, weight * (ints / (gaps[:, None] + own_gaps[None, :])), 0.0)
    return lax.all_gather(amplitude, "aux", axis=0, tiled=True)


def term(far, amplitude):
    return jnp.dot(far, amplitude, precision=PRECISE, preferred_element_type=jnp.float32)


def local_ring(factors, eps_occ, eps_vir, tile_index, pair_offset):
    count = lax.axis_size("occ")
    me = lax.axis_index("occ")
    vir_energy = lax.dynamic_slice_in_dim(eps_vir, tile_index[0] * VT, VT)
    energy = eps_occ.reshape(count, BLK)
    own_gaps = gaps_of(vir_energy, energy[me])
    offset = pair_offset[0]
    total = jnp.zeros_like(factors)
    for sign in (1, -1):
        far = factors
        held = factors
        for hop in range(1, DMAX + 1):
            held = lax.ppermute(held, "occ", [(i, (i + sign) % count) for i in range(count)])
            far = jnp.where(offset == hop, held, far)
        far_gaps = gaps_of(vir_energy, energy[(me - sign * offset) % count])
        total = total + term(far, amplitude_of(factors, far, own_gaps, far_gaps, jnp.float32(1)))
    return total


def split(x):
    high = x.astype(jnp.bfloat16)
    return high, (x - high.astype(jnp.float32)).astype(jnp.bfloat16)


def dot3(left, right, dims):
    dot = functools.partial(lax.dot_general, dimension_numbers=(dims, ((), ())), preferred_element_type=jnp.float32)
    return dot(left[0], right[0]) + (dot(left[0], right[1]) + dot(left[1], right[0]))


def line_kernel(
    occ, aux, own, offset, table, total_out, far_out, amp_out, out,
    near, other, across, relay, own_hi, own_lo, far_hi, far_lo,
    ints, core_in, half, x_in, amp, own_row, gap_cols,
    near_s, near_r, other_s, other_r, fwd_s, relay_s, across_r,
    a_s, a_r, b_s, b_r, c_s, c_r, out_s,
):
    chunks, rows, width = near.shape
    tile_width = own.shape[1]
    share = width // 2
    band = rows // PARTS
    me = lax.axis_index("occ")
    rank = lax.axis_index("aux")
    inner = jnp.logical_and(me > 0, me < occ - 1)
    side = {"occ": me + 1 - 2 * (me % 2)}
    middle = {"occ": occ - 1 - me}
    core = {"aux": rank + 1 - 2 * (rank % 2)}
    xpeer = {"aux": (rank + 2) % aux}
    mine = pl.multiple_of((rank % 2) * share, share)
    theirs = pl.multiple_of((1 - rank % 2) * share, share)

    def remote(src, dst, send, recv, target):
        return pltpu.make_async_remote_copy(
            src_ref=src, dst_ref=dst, send_sem=send, recv_sem=recv, device_id=target, device_id_type=MESH
        )

    def columns(c):
        return pl.ds(pl.multiple_of(c * width, width), width)

    def near_copy(c):
        return remote(own.at[:, columns(c)], near.at[c], near_s.at[c], near_r.at[c], side)

    def other_copy(c):
        return remote(own.at[:, columns(c)], other.at[c], other_s.at[c], other_r.at[c], middle)

    def band_of(t):
        return pl.ds(pl.multiple_of(t * band, band), band)

    def forward_copy(c, t):
        span = band_of(t)
        return remote(near.at[c, span], across.at[c, span], fwd_s.at[c, t], across_r.at[c, t], middle)

    def relay_copy(c, t):
        span = band_of(t)
        return remote(relay.at[c, span], across.at[c, span], relay_s.at[c, t], across_r.at[c, t], side)

    def a_copy(i):
        return remote(ints.at[i, pl.ds(theirs, share)], core_in.at[i], a_s.at[i], a_r.at[i], core)

    def b_copy(i):
        return remote(half.at[i], x_in.at[i], b_s.at[i], b_r.at[i], xpeer)

    def c_copy(i):
        rows_of = amp.at[i, pl.ds(mine, share)]
        return remote(rows_of, rows_of, c_s.at[i], c_r.at[i], core)

    barrier = pltpu.get_barrier_semaphore()
    for target in (side, core, xpeer):
        pl.semaphore_signal(barrier, inc=1, device_id=target, device_id_type=MESH)

    @pl.when(inner)
    def _():
        pl.semaphore_signal(barrier, inc=1, device_id=middle, device_id_type=MESH)
        pl.semaphore_wait(barrier, 4)

    @pl.when(jnp.logical_not(inner))
    def _():
        pl.semaphore_wait(barrier, 3)

    @pl.loop(0, chunks)
    def _(c):
        near_copy(c).start()

        @pl.when(inner)
        def _():
            other_copy(c).start()

    items = 2 * chunks
    odd = offset[0] & 1

    @pl.loop(0, PARTS)
    def _(t):
        span = band_of(t)
        own_hi[span, :], own_lo[span, :] = split(own[span, :])
        out[span, :] = jnp.zeros((band, tile_width), jnp.float32)

    for r in range(chunks):
        own_row[:, r * width : (r + 1) * width] = table[r : r + 1, :]

    @pl.loop(0, items)
    def _(i):
        gap_cols[i] = jnp.broadcast_to(table[pl.ds(chunks + i, 1), :], (width, width)).T

    def pick(odd_one, even_one):
        return jnp.where(jnp.full((band, width), odd, jnp.int32) > 0, odd_one, even_one)

    def integrals(i, slot, t, far):
        span = band_of(t)
        parts = split(far)
        far_hi[slot, span, :], far_lo[slot, span, :] = parts

        @pl.when(i == items - 1)
        def _():
            far_out[span, :] = far

        for n in range(0, tile_width, NTILE):
            cols = slice(n, n + NTILE)
            ints[i, :, cols] += dot3(parts, (own_hi[span, cols], own_lo[span, cols]), ((0,), (0,)))

    def serve(c, t):
        @pl.when(inner)
        def _():
            if t == 0:
                other_copy(c).wait_recv()
            forward_copy(c, t).wait_recv()
            span = band_of(t)
            relay[c, span, :] = pick(across[c, span, :], other[c, span, :])
            relay_copy(c, t).start()
            i = c + chunks
            if t == 0:
                ints[i] = jnp.zeros((width, tile_width), jnp.float32)
            integrals(i, i % SLOTS, t, pick(other[c, span, :], across[c, span, :]))

    def serve_next(i, t):
        @pl.when(jnp.logical_and(i >= chunks - 1, i < items - 1))
        def _():
            serve(i + 1 - chunks, t)

    def front(i, slot):
        c = i % chunks

        @pl.when(i < chunks)
        def _():
            ints[i] = jnp.zeros((width, tile_width), jnp.float32)
            near_copy(c).wait_recv()

            @pl.when(inner)
            def _():
                @pl.loop(0, PARTS)
                def _(t):
                    forward_copy(c, t).start()

            @pl.loop(0, PARTS)
            def _(t):
                integrals(i, slot, t, near[c, band_of(t), :])

        @pl.when(i >= chunks)
        def _():
            serve(c, PARTS - 1)

            @pl.when(jnp.logical_not(inner))
            def _():
                ints[i] = jnp.zeros((width, tile_width), jnp.float32)

                @pl.loop(0, PARTS)
                def _(t):
                    relay_copy(c, t).wait_recv()
                    integrals(i, slot, t, across[c, band_of(t), :])

        a_copy(i).start()

    @pl.loop(0, items + 1)
    def _(i):
        slot, back = i % SLOTS, (i + SLOTS - 1) % SLOTS

        @pl.when(i == items)
        def _():
            pltpu.make_async_copy(out, total_out, out_s).start()

        @pl.when(i < items)
        def _():
            front(i, slot)

        serve_next(i, 0)

        @pl.when(i > 0)
        def _():
            j = i - 1
            b_copy(j).wait_recv()
            at = pl.ds(mine, share)
            single = jnp.full((share, width), odd, jnp.int32).astype(jnp.float32)
            weight = jnp.where(j < chunks, single, 2.0 - single)
            for r in range(chunks):
                cols = slice(r * width, (r + 1) * width)
                total = half[j, :, cols] + x_in[j, :, cols]
                amp[j, at, cols] = weight * (total / (gap_cols[j, at, :] + own_row[:, cols]))
            c_copy(j).start()

        @pl.when(i < items)
        def _():
            a_copy(i).wait_recv()
            half[i] = ints[i, pl.ds(mine, share), :] + core_in[i]
            b_copy(i).start()

        serve_next(i, 1)

        @pl.when(i > 0)
        def _():
            j = i - 1
            c_copy(j).wait_recv()

        def add_terms(first, last):
            @pl.when(jnp.logical_and(i > 0, i < items))
            def _():
                amp_parts = split(amp[i - 1])

                @pl.loop(first, last)
                def _(t):
                    span = band_of(t)
                    out[span, :] += dot3((far_hi[back, span, :], far_lo[back, span, :]), amp_parts, ((1,), (0,)))

        add_terms(0, PARTS // 2)
        serve_next(i, 2)
        add_terms(PARTS // 2, PARTS)

    amp_out[...] = amp[items - 1]
    pltpu.make_async_copy(out, total_out, out_s).wait()

    @pl.loop(0, chunks)
    def _(c):
        near_copy(c).wait_send()

        @pl.when(inner)
        def _():
            other_copy(c).wait_send()

            @pl.loop(0, PARTS)
            def _(t):
                forward_copy(c, t).wait_send()
                relay_copy(c, t).wait_send()

    @pl.loop(0, items)
    def _(i):
        a_copy(i).wait_send()
        b_copy(i).wait_send()
        c_copy(i).wait_send()


def local_line(factors, eps_occ, eps_vir, tile_index, pair_offset):
    count = lax.axis_size("occ")
    aux_count = lax.axis_size("aux")
    me = lax.axis_index("occ")
    rows, tile_width = factors.shape
    vir_energy = lax.dynamic_slice_in_dim(eps_vir, tile_index[0] * VT, VT)
    energy = eps_occ.reshape(count, BLK)
    odd = pair_offset[0] % 2 == 1
    near_block = me + 1 - 2 * (me % 2)
    far_block = jnp.where(odd, jnp.where(me % 2 == 0, me - 1, me + 1), me + 2) % count
    blocks = jnp.stack([energy[me], energy[near_block], energy[far_block]]).reshape(3 * BLK)
    table = gaps_of(vir_energy, blocks).reshape(3 * tile_width // WIDTH, WIDTH)
    chunks = tile_width // WIDTH
    items = 2 * chunks
    f32, half = jnp.float32, jnp.bfloat16
    block = pltpu.VMEM((chunks, rows, WIDTH), f32)
    share = pltpu.VMEM((items, WIDTH // 2, tile_width), f32)
    dma = pltpu.SemaphoreType.DMA
    vmem = pl.BlockSpec(memory_space=pltpu.VMEM)
    total, far, amplitude = pl.pallas_call(
        functools.partial(line_kernel, count, aux_count),
        out_shape=[
            jax.ShapeDtypeStruct((rows, tile_width), f32),
            jax.ShapeDtypeStruct((rows, WIDTH), f32),
            jax.ShapeDtypeStruct((WIDTH, tile_width), f32),
        ],
        in_specs=[vmem, pl.BlockSpec(memory_space=pltpu.SMEM), vmem],
        out_specs=[pl.BlockSpec(memory_space=pl.ANY), vmem, vmem],
        scratch_shapes=[pltpu.VMEM((rows, tile_width), f32)]
        + [block] * 4
        + [pltpu.VMEM((rows, tile_width), half)] * 2
        + [pltpu.VMEM((SLOTS, rows, WIDTH), half)] * 2
        + [pltpu.VMEM((items, WIDTH, tile_width), f32), share, share, share]
        + [pltpu.VMEM((items, WIDTH, tile_width), f32)]
        + [pltpu.VMEM((1, tile_width), f32), pltpu.VMEM((items, WIDTH, WIDTH), f32)]
        + [dma((chunks,))] * 4
        + [dma((chunks, PARTS))] * 3
        + [dma((items,))] * 6
        + [dma],
        compiler_params=pltpu.CompilerParams(
            collective_id=0, has_side_effects=True, vmem_limit_bytes=56 * 1024 * 1024
        ),
        name="pair_line",
    )(factors, pair_offset, table)
    return total + term(far, amplitude)


def solution(mesh):
    in_specs = (P(("grp", "aux"), "occ"), P("grp"), P("grp"), P("grp"), P("grp"))
    out_specs = P(("grp", "aux"), "occ")
    body = local_line if mesh.shape["occ"] == LINE and mesh.shape["aux"] == SHARDS else local_ring
    return jax.shard_map(body, mesh=mesh, in_specs=in_specs, out_specs=out_specs, check_vma=False)
```
